256 devices in a mesh: dp: 4 (over y), expert: 64 (over x, z, core).
Axes of the slice: x: 4, y: 4, z: 8, core: 2. Of those that a mesh axis runs over, the one named last changes fastest.
Arguments:
- tokens: bfloat16 [8192, 7168], P('expert', 'dp'), may hold values from -6 to 6
- route_ids: int32 [8192, 8], P('expert'), may hold values from 0 to 63, all different within a row; in each aligned block of 128 rows (0 to 127, 128 to 255, ...) at most 20 rows name the same one
- route_weights: float32 [8192, 8], P('expert'), may hold values from 0.1 to 0.6
- swap_flags: int32 [64], replicated, may hold values from 0 to 1, as said below
- gate_weight: bfloat16 [64, 7168, 1024], P('expert', 'dp'), may hold values from -0.0625 to 0.0625
- up_weight: bfloat16 [64, 7168, 1024], P('expert', 'dp'), may hold values from -0.0625 to 0.0625
- down_weight: bfloat16 [64, 1024, 7168], P('expert', None, 'dp'), may hold values from -0.1875 to 0.1875
Outputs:
- mixed: bfloat16 [8192, 7168], P('expert', 'dp')
The draws below stay inside these ranges and needn't reach their ends.
Inputs may be any that keep to these rules, and one draw needn't show every extreme that they name: `route_ids`: each row names 8 different slots. In each aligned block of 128 rows (the rows of one device along `expert`) no slot is named by more than 20 rows, a bound that some block reaches. swap_flags[s] equals swap_flags[(s + 32) mod 64] for every slot s; swap_flags[0] and swap_flags[31] are 1 and swap_flags[1] is 0.
All inputs are finite; a program needn't handle non-finite values.
Results may differ from the reference program's by a relative error of at most 0.019.
Values may be sent and summed in bfloat16 or wider, within the bound.
No kernel may reach another device: no remote copies, remote signals or barrier semaphores. Data moves between devices by JAX's collectives and lax.ppermute only.
A program may use at most 128 MiB of HBM per device.

```python
import math
import jax
import jax.numpy as jnp
import numpy as np
from jax import lax

D = 7168
H = 1024
K = 8
TOK_DEV = 128
EXPERTS = 64
TOKENS = 8192
CAP = 20
N_DP = 4


def draw_swap_flags(key, part):
    half_count = EXPERTS // 2
    raw_bits = jax.random.randint(jax.random.fold_in(key, 40503), (half_count,), 0, 2).astype(jnp.int32)
    paired_bits = raw_bits.at[0].set(1)
    paired_bits = paired_bits.at[1].set(0)
    paired_bits = paired_bits.at[half_count - 1].set(1)
    return jnp.concatenate([paired_bits, paired_bits]).astype(jnp.int32)


def block_scale(key, extent, split, least, largest):
    def one(dim, shards_of):
        steps = jax.random.uniform(jax.random.fold_in(jax.random.fold_in(key, 6), dim), (shards_of,), jnp.float32, least / len(split), largest / len(split))
        return jnp.repeat(jnp.exp(steps), extent[dim] // shards_of).reshape((-1,) + (1,) * (len(extent) - dim - 1))

    level = one(*split[0])
    for cut in split[1:]:
        level = level * one(*cut)
    return level


def deal_out(rng, own, number, rows, number_of, top, most, skew):
    order = jax.random.permutation(rng, number_of)
    packed, ordinary = portions_of(number_of, rows * top, most, skew, True), portions_of(number_of, rows * top, most, skew, False)
    places = jnp.arange(number_of)

    def named(tallies, offset_by):
        used = int((tallies > 0).sum())
        fixed = max(1, used // 4)
        moved = fixed + (places - fixed + offset_by * (used - fixed)) % max(1, number_of - fixed)
        return jnp.zeros((number_of,), jnp.int32).at[order[jnp.where(places < fixed, places, moved)]].set(jnp.asarray(tallies, jnp.int32))

    tallies = jnp.where(number % 4 == 0, named(packed, number // 4), named(ordinary, number - number // 4 - 1))
    mixed = jax.random.permutation(jax.random.fold_in(own, 3), number_of)
    giver, taker = mixed[0:number_of // 2 * 2:2], mixed[1:number_of // 2 * 2:2]
    margin = jnp.minimum(tallies[giver] - 1, most - tallies[taker]) // 2
    margin = jnp.where((giver == order[0]) | (taker == order[0]) | (tallies[taker] == 0), 0, jnp.maximum(margin, 0))
    moved = jax.random.randint(jax.random.fold_in(own, 4), (number_of // 2,), 0, 1 << 20) % (margin + 1)
    tallies = tallies.at[giver].add(-moved).at[taker].add(moved)
    labels = jnp.searchsorted(jnp.cumsum(tallies), jnp.arange(rows * top), side="right").astype(jnp.int32)
    table = labels.reshape(top, rows).T
    table = table[jax.random.permutation(jax.random.fold_in(own, 1), rows)]
    offset_by = jax.random.randint(jax.random.fold_in(own, 2), (rows, 1), 0, top)
    return jnp.take_along_axis(table, (jnp.arange(top)[None, :] + offset_by) % top, axis=1)


def portions_of(number_of, total, reach, skew, full):
    loads = [(1 << 20) // math.isqrt(rank ** skew) + 1 for rank in range(1, number_of + 1)]
    largest = reach if full else min(reach, max(-(-total // number_of), total * loads[0] // sum(loads)))
    least = 1 if total - largest >= number_of - 1 else 0
    counts, rest = [largest] + [least] * (number_of - 1), total - largest - least * (number_of - 1)
    while rest > 0:
        free = [i for i in range(1, number_of) if counts[i] < largest] or [i for i in range(1, number_of) if counts[i] < reach]
        mass, remaining = sum([loads[i] for i in free]), rest
        for i in free:
            addition = min(reach - counts[i], max(1, remaining * loads[i] // mass), rest)
            counts[i] = counts[i] + addition
            rest = rest - addition
    return np.array(counts)


def gaussian(key, extent, spread, most, cuts=(), kind=jnp.bfloat16):
    result = jax.random.normal(key, extent, jnp.float32) * spread
    if len(cuts) > 0:
        result = block_scale(key, extent, cuts, -0.22, 0.18) * result
    return jnp.clip(result, min=-most, max=most).astype(kind)


def setup_inputs(seed: int = 0) -> dict:
    key_of = jax.random.split(jax.random.key(seed), 8)
    tokens = gaussian(key_of[0], (TOKENS, D), 1.0, 6.0, ((0, 64), (1, 4)))
    route_ids_keys = jax.random.split(jax.random.fold_in(key_of[1], 1), TOKENS // TOK_DEV)
    route_ids_turns = jax.random.permutation(jax.random.fold_in(key_of[1], 3), TOKENS // TOK_DEV)
    route_ids = jax.vmap(lambda own, number: deal_out(jax.random.fold_in(key_of[1], 2), own, number, TOK_DEV, EXPERTS, K, CAP, 2))(route_ids_keys, route_ids_turns).reshape((TOKENS, K))
    route_weights = jnp.clip(0.1 + 0.5 * jax.random.uniform(key_of[2], (TOKENS, K), jnp.float32) ** block_scale(key_of[2], (TOKENS, K), ((0, 64),), -0.2, 0.2), 0.1, 0.6)
    swap_flags = draw_swap_flags(jax.random.fold_in(key_of[7], 71), 0)
    gate_weight = gaussian(key_of[4], (EXPERTS, D, H), D ** -0.5, 0.0625, ((0, 64), (1, 4)))
    up_weight = gaussian(key_of[5], (EXPERTS, D, H), D ** -0.5, 0.0625, ((0, 64), (1, 4)))
    down_weight = gaussian(key_of[6], (EXPERTS, H, D), H ** -0.5, 0.1875, ((0, 64), (2, 4)))
    return dict(tokens=tokens, route_ids=route_ids, route_weights=route_weights, swap_flags=swap_flags, gate_weight=gate_weight, up_weight=up_weight, down_weight=down_weight)


def rounded_sum(row_block, weight_block):
    quarter = D // N_DP
    total_sum = jnp.zeros((row_block.shape[0], weight_block.shape[1]), jnp.float32)
    for quarter_index in range(N_DP):
        column_start = quarter_index * quarter
        partial_term = jnp.dot(row_block[:, column_start:column_start + quarter], weight_block[column_start:column_start + quarter], preferred_element_type=jnp.float32).astype(jnp.bfloat16)
        total_sum = total_sum + lax.optimization_barrier(partial_term).astype(jnp.float32)
    return total_sum


def reference(tokens, route_ids, route_weights, swap_flags, gate_weight, up_weight, down_weight):
    slot_ids = jnp.arange(EXPERTS, dtype=jnp.int32)
    slot_source = jnp.where(swap_flags == 1, (slot_ids + EXPERTS // 2) % EXPERTS, slot_ids).astype(jnp.int32)
    flat_ids = route_ids.reshape(-1).astype(jnp.int32)
    entries = flat_ids.shape[0]
    sort_order = jnp.argsort(flat_ids, stable=True).astype(jnp.int32)
    slot_counts = jnp.sum((flat_ids[:, None] == slot_ids[None, :]).astype(jnp.int32), axis=0)
    slot_starts = (jnp.cumsum(slot_counts) - slot_counts).astype(jnp.int32)
    flat_weights = route_weights.reshape(-1)
    most_rows = EXPERTS * CAP

    def one_expert(expert_index, mixed_sum):
        offsets = jnp.arange(most_rows, dtype=jnp.int32)
        live_rows = offsets < slot_counts[expert_index]
        entry_ids = sort_order[jnp.minimum(slot_starts[expert_index] + offsets, entries - 1)]
        token_ids = (entry_ids // K).astype(jnp.int32)
        gathered = tokens[token_ids]
        row_block = jnp.where(live_rows[:, None], gathered, jnp.zeros_like(gathered))
        owner_slot = slot_source[expert_index]
        gate_sum = rounded_sum(row_block, gate_weight[owner_slot])
        up_sum = rounded_sum(row_block, up_weight[owner_slot])
        activated = (jax.nn.silu(gate_sum) * up_sum).astype(jnp.bfloat16)
        expert_out = jnp.dot(activated, down_weight[owner_slot], preferred_element_type=jnp.float32).astype(jnp.bfloat16)
        row_weight = jnp.where(live_rows, flat_weights[entry_ids], jnp.zeros_like(flat_weights[entry_ids]))
        return mixed_sum.at[token_ids].add(row_weight[:, None] * expert_out.astype(jnp.float32))

    mixed_sum = lax.fori_loop(0, EXPERTS, one_expert, jnp.zeros((tokens.shape[0], D), jnp.float32))
    return mixed_sum.astype(jnp.bfloat16)
```

```python
import jax
import jax.numpy as jnp
from jax import lax
from jax.sharding import PartitionSpec as P


def shifted(x, axis, by):
    devices = lax.axis_size(axis)
    return lax.ppermute(x, axis, [(i, (i + by) % devices) for i in range(devices)])


def per_device(tokens, route_ids, route_weights, swap_flags, gate_weight, up_weight, down_weight):
    experts = lax.axis_size("expert")
    tok_rows, quarter = tokens.shape
    choices_per = route_ids.shape[1]
    hidden = gate_weight.shape[2]
    capacity = max(2, min(tok_rows, 5 * tok_rows * choices_per // (4 * experts)))
    w_gate = gate_weight[0]
    w_up = up_weight[0]
    w_down = down_weight[0]
    slots = jnp.arange(experts, dtype=jnp.int32)
    slot_source = jnp.where(swap_flags == 1, (slots + experts // 2) % experts, slots)
    flat_ids = slot_source[route_ids.reshape(-1)]
    onehot = (flat_ids[:, None] == jnp.arange(experts, dtype=jnp.int32)[None, :]).astype(jnp.int32)
    running = jnp.cumsum(onehot, axis=0) - onehot
    rank_in = jnp.sum(running * onehot, axis=1)
    slot_of = flat_ids * capacity + rank_in
    entry_count = flat_ids.shape[0]
    slot_table = (
        jnp.zeros((experts * capacity,), jnp.int32)
        .at[slot_of]
        .set(jnp.arange(entry_count, dtype=jnp.int32) + 1)
    )
    filled = slot_table > 0
    source_tok = jnp.maximum(slot_table - 1, 0) // choices_per
    gathered = tokens[source_tok]
    outgoing = jnp.where(filled[:, None], gathered, jnp.zeros_like(gathered)).reshape(
        experts, capacity, quarter
    )
    arrived = lax.all_to_all(outgoing, "expert", split_axis=0, concat_axis=0, tiled=True)
    all_rows = arrived.reshape(experts * capacity, quarter)
    gate_term = jnp.dot(all_rows, w_gate, preferred_element_type=jnp.float32)
    up_term = jnp.dot(all_rows, w_up, preferred_element_type=jnp.float32)
    summed = lax.psum_scatter(
        jnp.concatenate([gate_term, up_term], axis=1).astype(jnp.bfloat16),
        "dp",
        scatter_dimension=0,
        tiled=True,
    ).astype(jnp.float32)
    activated = (jax.nn.silu(summed[:, :hidden]) * summed[:, hidden:]).astype(jnp.bfloat16)
    results = jnp.dot(
        lax.all_gather(activated, "dp", axis=0, tiled=True),
        w_down,
        preferred_element_type=jnp.float32,
    )
    leaving = results.astype(jnp.bfloat16).reshape(experts, capacity, quarter)
    returned = lax.all_to_all(leaving, "expert", split_axis=0, concat_axis=0, tiled=True)
    returned_flat = returned.reshape(experts * capacity, quarter)
    picked = returned_flat[slot_of].reshape(tok_rows, choices_per, quarter)
    mixed = jnp.sum(route_weights[:, :, None] * picked.astype(jnp.float32), axis=1)
    return mixed.astype(jnp.bfloat16)


def solution(mesh):
    in_specs = (
        P("expert", "dp"),
        P("expert", None),
        P("expert", None),
        P(),
        P("expert", "dp", None),
        P("expert", "dp", None),
        P("expert", None, "dp"),
    )
    out_specs = P("expert", "dp")
    return jax.shard_map(
        per_device, mesh=mesh, in_specs=in_specs, out_specs=out_specs, check_vma=False
    )
```

```python
import jax
import jax.numpy as jnp
from jax import lax
from jax.sharding import PartitionSpec as P


def per_device(tokens, route_ids, route_weights, swap_flags, gate_weight, up_weight, down_weight):
    experts = lax.axis_size("expert")
    tok_rows, quarter = tokens.shape
    choices_per = route_ids.shape[1]
    hidden = gate_weight.shape[2]
    capacity = max(2, min(tok_rows, 5 * tok_rows * choices_per // (4 * experts)))
    w_gate = gate_weight[0]
    w_up = up_weight[0]
    w_down = down_weight[0]
    entries = tok_rows * choices_per
    flat_ids = route_ids.reshape(-1)
    slots = jnp.arange(experts, dtype=jnp.int32)
    onehot = flat_ids[:, None] == slots[None, :]
    entry_ids = jnp.arange(entries, dtype=jnp.int32)
    earlier = (entry_ids[:, None] > entry_ids[None, :]).astype(jnp.bfloat16)
    running = jnp.dot(earlier, onehot.astype(jnp.bfloat16), preferred_element_type=jnp.float32)
    rank_in = jnp.sum(jnp.where(onehot, running, 0.0), axis=1).astype(jnp.int32)
    flag = jnp.sum(jnp.where(onehot, swap_flags[None, :], 0), axis=1)
    home = jnp.where(flag == 1, (flat_ids + experts // 2) % experts, flat_ids)
    slot_of = (home * capacity + rank_in).reshape(tok_rows, choices_per)
    positions = jnp.arange(experts * capacity, dtype=jnp.int32)
    hit = slot_of[:, :, None] == positions[None, None, :]
    pick = jnp.any(hit, axis=1).astype(jnp.bfloat16)
    outgoing = lax.dot_general(
        pick, tokens, (((0,), (0,)), ((), ())), preferred_element_type=jnp.float32
    ).astype(jnp.bfloat16)
    arrived = lax.all_to_all(
        outgoing.reshape(experts, capacity, quarter), "expert", split_axis=0, concat_axis=0, tiled=True
    )
    all_rows = arrived.reshape(experts * capacity, quarter)
    gate_term = jnp.dot(all_rows, w_gate, preferred_element_type=jnp.float32)
    up_term = jnp.dot(all_rows, w_up, preferred_element_type=jnp.float32)
    summed = lax.psum_scatter(
        jnp.concatenate([gate_term, up_term], axis=1).astype(jnp.bfloat16),
        "dp",
        scatter_dimension=0,
        tiled=True,
    ).astype(jnp.float32)
    activated = (jax.nn.silu(summed[:, :hidden]) * summed[:, hidden:]).astype(jnp.bfloat16)
    results = jnp.dot(
        lax.all_gather(activated, "dp", axis=0, tiled=True),
        w_down,
        preferred_element_type=jnp.float32,
    )
    leaving = results.astype(jnp.bfloat16).reshape(experts, capacity, quarter)
    returned = lax.all_to_all(leaving, "expert", split_axis=0, concat_axis=0, tiled=True)
    returned_flat = returned.reshape(experts * capacity, quarter)
    weight_of = jnp.sum(jnp.where(hit, route_weights[:, :, None], 0.0), axis=1)
    weight_hi = weight_of.astype(jnp.bfloat16)
    weight_lo = (weight_of - weight_hi.astype(jnp.float32)).astype(jnp.bfloat16)
    mixed = jnp.dot(weight_hi, returned_flat, preferred_element_type=jnp.float32) + jnp.dot(
        weight_lo, returned_flat, preferred_element_type=jnp.float32
    )
    return mixed.astype(jnp.bfloat16)


def solution(mesh):
    in_specs = (
        P("expert", "dp"),
        P("expert", None),
        P("expert", None),
        P(),
        P("expert", "dp", None),
        P("expert", "dp", None),
        P("expert", None, "dp"),
    )
    out_specs = P("expert", "dp")
    return jax.shard_map(
        per_device, mesh=mesh, in_specs=in_specs, out_specs=out_specs, check_vma=False
    )
```

```python
import jax
import jax.numpy as jnp
from jax import lax
from jax.sharding import PartitionSpec as P


def per_device(tokens, route_ids, route_weights, swap_flags, gate_weight, up_weight, down_weight):
    experts = lax.axis_size("expert")
    tok_rows, quarter = tokens.shape
    choices_per = route_ids.shape[1]
    hidden = gate_weight.shape[2]
    capacity = max(2, min(tok_rows, 5 * tok_rows * choices_per // (4 * experts)))
    w_gate = gate_weight[0]
    w_up = up_weight[0]
    w_down = down_weight[0]
    entries = tok_rows * choices_per
    flat_ids = route_ids.reshape(-1)
    slots = jnp.arange(experts, dtype=jnp.int32)
    onehot = flat_ids[:, None] == slots[None, :]
    entry_ids = jnp.arange(entries, dtype=jnp.int32)
    earlier = (entry_ids[:, None] > entry_ids[None, :]).astype(jnp.bfloat16)
    running = jnp.dot(earlier, onehot.astype(jnp.bfloat16), preferred_element_type=jnp.float32)
    rank_in = jnp.sum(jnp.where(onehot, running, 0.0), axis=1).astype(jnp.int32)
    flag = jnp.sum(jnp.where(onehot, swap_flags[None, :], 0), axis=1)
    home = jnp.where(flag == 1, (flat_ids + experts // 2) % experts, flat_ids)
    slot_of = (home * capacity + rank_in).reshape(tok_rows, choices_per)
    positions = jnp.arange(experts * capacity, dtype=jnp.int32)
    hit = slot_of[:, :, None] == positions[None, None, :]
    pick = jnp.any(hit, axis=1).astype(jnp.bfloat16)
    outgoing = lax.dot_general(
        pick, tokens, (((0,), (0,)), ((), ())), preferred_element_type=jnp.float32
    ).astype(jnp.bfloat16)
    lane = 128
    packed = (experts, capacity * quarter // lane, lane)
    arrived = lax.all_to_all(outgoing.reshape(packed), "expert", split_axis=0, concat_axis=0, tiled=True)
    all_rows = arrived.reshape(experts * capacity, quarter)
    gate_term = jnp.dot(all_rows, w_gate, preferred_element_type=jnp.float32)
    up_term = jnp.dot(all_rows, w_up, preferred_element_type=jnp.float32)
    summed = lax.psum_scatter(
        jnp.concatenate([gate_term, up_term], axis=1).astype(jnp.bfloat16),
        "dp",
        scatter_dimension=0,
        tiled=True,
    ).astype(jnp.float32)
    activated = (jax.nn.silu(summed[:, :hidden]) * summed[:, hidden:]).astype(jnp.bfloat16)
    results = jnp.dot(
        lax.all_gather(activated, "dp", axis=0, tiled=True),
        w_down,
        preferred_element_type=jnp.float32,
    )
    leaving = results.astype(jnp.bfloat16).reshape(packed)
    returned = lax.all_to_all(leaving, "expert", split_axis=0, concat_axis=0, tiled=True)
    returned_flat = returned.reshape(experts * capacity, quarter)
    weight_of = jnp.sum(jnp.where(hit, route_weights[:, :, None], 0.0), axis=1)
    weight_hi = weight_of.astype(jnp.bfloat16)
    weight_lo = (weight_of - weight_hi.astype(jnp.float32)).astype(jnp.bfloat16)
    mixed = jnp.dot(weight_hi, returned_flat, preferred_element_type=jnp.float32) + jnp.dot(
        weight_lo, returned_flat, preferred_element_type=jnp.float32
    )
    return mixed.astype(jnp.bfloat16)


def solution(mesh):
    in_specs = (
        P("expert", "dp"),
        P("expert", None),
        P("expert", None),
        P(),
        P("expert", "dp", None),
        P("expert", "dp", None),
        P("expert", None, "dp"),
    )
    out_specs = P("expert", "dp")
    return jax.shard_map(
        per_device, mesh=mesh, in_specs=in_specs, out_specs=out_specs, check_vma=False
    )
```

```python
import jax
import jax.numpy as jnp
from jax import lax
from jax.sharding import PartitionSpec as P


def expert_rows(rows, w_gate, w_up, w_down, hidden):
    gate_term = jnp.dot(rows, w_gate, preferred_element_type=jnp.float32)
    up_term = jnp.dot(rows, w_up, preferred_element_type=jnp.float32)
    summed = lax.psum_scatter(
        jnp.concatenate([gate_term, up_term], axis=1).astype(jnp.bfloat16),
        "dp",
        scatter_dimension=0,
        tiled=True,
    ).astype(jnp.float32)
    activated = (jax.nn.silu(summed[:, :hidden]) * summed[:, hidden:]).astype(jnp.bfloat16)
    results = jnp.dot(
        lax.all_gather(activated, "dp", axis=0, tiled=True),
        w_down,
        preferred_element_type=jnp.float32,
    )
    return results.astype(jnp.bfloat16)


def per_device(tokens, route_ids, route_weights, swap_flags, gate_weight, up_weight, down_weight):
    experts = lax.axis_size("expert")
    tok_rows, quarter = tokens.shape
    choices_per = route_ids.shape[1]
    hidden = gate_weight.shape[2]
    capacity = max(2, min(tok_rows, 5 * tok_rows * choices_per // (4 * experts)))
    w_gate = gate_weight[0]
    w_up = up_weight[0]
    w_down = down_weight[0]
    entries = tok_rows * choices_per
    flat_ids = route_ids.reshape(-1)
    slots = jnp.arange(experts, dtype=jnp.int32)
    onehot = flat_ids[:, None] == slots[None, :]
    entry_ids = jnp.arange(entries, dtype=jnp.int32)
    earlier = (entry_ids[:, None] > entry_ids[None, :]).astype(jnp.bfloat16)
    running = jnp.dot(earlier, onehot.astype(jnp.bfloat16), preferred_element_type=jnp.float32)
    rank_in = jnp.sum(jnp.where(onehot, running, 0.0), axis=1).astype(jnp.int32)
    flag = jnp.sum(jnp.where(onehot, swap_flags[None, :], 0), axis=1)
    home = jnp.where(flag == 1, (flat_ids + experts // 2) % experts, flat_ids)
    home = home.reshape(tok_rows, choices_per)
    rank_in = rank_in.reshape(tok_rows, choices_per)
    pieces = 2 if capacity % 2 == 0 else 1
    share = capacity // pieces
    lane = 128
    packed = (experts, share * quarter // lane, lane)
    positions = jnp.arange(experts * share, dtype=jnp.int32)
    mixed = jnp.zeros((tok_rows, quarter), jnp.float32)
    for piece in range(pieces):
        inside = (rank_in >= piece * share) & (rank_in < (piece + 1) * share)
        slot_of = jnp.where(inside, home * share + rank_in - piece * share, -1)
        hit = slot_of[:, :, None] == positions[None, None, :]
        pick = jnp.any(hit, axis=1).astype(jnp.bfloat16)
        outgoing = lax.dot_general(
            pick, tokens, (((0,), (0,)), ((), ())), preferred_element_type=jnp.float32
        ).astype(jnp.bfloat16)
        arrived = lax.all_to_all(outgoing.reshape(packed), "expert", split_axis=0, concat_axis=0, tiled=True)
        served = expert_rows(arrived.reshape(experts * share, quarter), w_gate, w_up, w_down, hidden)
        returned = lax.all_to_all(served.reshape(packed), "expert", split_axis=0, concat_axis=0, tiled=True)
        returned_flat = returned.reshape(experts * share, quarter)
        weight_of = jnp.sum(jnp.where(hit, route_weights[:, :, None], 0.0), axis=1)
        weight_hi = weight_of.astype(jnp.bfloat16)
        weight_lo = (weight_of - weight_hi.astype(jnp.float32)).astype(jnp.bfloat16)
        mixed = mixed + jnp.dot(weight_hi, returned_flat, preferred_element_type=jnp.float32)
        mixed = mixed + jnp.dot(weight_lo, returned_flat, preferred_element_type=jnp.float32)
    return mixed.astype(jnp.bfloat16)


def solution(mesh):
    in_specs = (
        P("expert", "dp"),
        P("expert", None),
        P("expert", None),
        P(),
        P("expert", "dp", None),
        P("expert", "dp", None),
        P("expert", None, "dp"),
    )
    out_specs = P("expert", "dp")
    return jax.shard_map(
        per_device, mesh=mesh, in_specs=in_specs, out_specs=out_specs, check_vma=False
    )
```

```python
import jax
import jax.numpy as jnp
from jax import lax
from jax.sharding import PartitionSpec as P

from jax.experimental import pallas as pl


def gate_up_kernel(x_ref, wg_ref, wu_ref, o_ref):
    col = pl.program_id(0)
    width = wg_ref.shape[1]
    half = width * pl.num_programs(0)
    x = x_ref[...]
    gate = jnp.dot(x, wg_ref[...], preferred_element_type=jnp.float32)
    up = jnp.dot(x, wu_ref[...], preferred_element_type=jnp.float32)
    o_ref[:, pl.ds(pl.multiple_of(col * width, width), width)] = gate.astype(o_ref.dtype)
    o_ref[:, pl.ds(pl.multiple_of(half + col * width, width), width)] = up.astype(o_ref.dtype)


def gate_up(x, wg, wu, width=256):
    rows, depth = x.shape
    hidden = wg.shape[1]
    return pl.pallas_call(
        gate_up_kernel,
        grid=(hidden // width,),
        in_specs=[
            pl.BlockSpec((rows, depth), lambda c: (0, 0)),
            pl.BlockSpec((depth, width), lambda c: (0, c)),
            pl.BlockSpec((depth, width), lambda c: (0, c)),
        ],
        out_specs=pl.BlockSpec((rows, 2 * hidden), lambda c: (0, 0)),
        out_shape=jax.ShapeDtypeStruct((rows, 2 * hidden), jnp.bfloat16),
    )(x, wg, wu)


def expert_rows(rows, w_gate, w_up, w_down, hidden):
    summed = lax.psum_scatter(
        gate_up(rows, w_gate, w_up),
        "dp",
        scatter_dimension=0,
        tiled=True,
    ).astype(jnp.float32)
    activated = (jax.nn.silu(summed[:, :hidden]) * summed[:, hidden:]).astype(jnp.bfloat16)
    results = jnp.dot(
        lax.all_gather(activated, "dp", axis=0, tiled=True),
        w_down,
        preferred_element_type=jnp.float32,
    )
    return results.astype(jnp.bfloat16)


def per_device(tokens, route_ids, route_weights, swap_flags, gate_weight, up_weight, down_weight):
    experts = lax.axis_size("expert")
    tok_rows, quarter = tokens.shape
    choices_per = route_ids.shape[1]
    hidden = gate_weight.shape[2]
    capacity = max(2, min(tok_rows, 5 * tok_rows * choices_per // (4 * experts)))
    w_gate = gate_weight[0]
    w_up = up_weight[0]
    w_down = down_weight[0]
    entries = tok_rows * choices_per
    flat_ids = route_ids.reshape(-1)
    slots = jnp.arange(experts, dtype=jnp.int32)
    onehot = flat_ids[:, None] == slots[None, :]
    entry_ids = jnp.arange(entries, dtype=jnp.int32)
    earlier = (entry_ids[:, None] > entry_ids[None, :]).astype(jnp.bfloat16)
    running = jnp.dot(earlier, onehot.astype(jnp.bfloat16), preferred_element_type=jnp.float32)
    rank_in = jnp.sum(jnp.where(onehot, running, 0.0), axis=1).astype(jnp.int32)
    flag = jnp.sum(jnp.where(onehot, swap_flags[None, :], 0), axis=1)
    home = jnp.where(flag == 1, (flat_ids + experts // 2) % experts, flat_ids)
    home = home.reshape(tok_rows, choices_per)
    rank_in = rank_in.reshape(tok_rows, choices_per)
    pieces = 2 if capacity % 2 == 0 else 1
    share = capacity // pieces
    lane = 128
    packed = (experts, share * quarter // lane, lane)
    positions = jnp.arange(experts * share, dtype=jnp.int32)
    mixed = jnp.zeros((tok_rows, quarter), jnp.float32)
    for piece in range(pieces):
        inside = (rank_in >= piece * share) & (rank_in < (piece + 1) * share)
        slot_of = jnp.where(inside, home * share + rank_in - piece * share, -1)
        hit = slot_of[:, :, None] == positions[None, None, :]
        pick = jnp.any(hit, axis=1).astype(jnp.bfloat16)
        outgoing = lax.dot_general(
            pick, tokens, (((0,), (0,)), ((), ())), preferred_element_type=jnp.float32
        ).astype(jnp.bfloat16)
        arrived = lax.all_to_all(outgoing.reshape(packed), "expert", split_axis=0, concat_axis=0, tiled=True)
        served = expert_rows(arrived.reshape(experts * share, quarter), w_gate, w_up, w_down, hidden)
        returned = lax.all_to_all(served.reshape(packed), "expert", split_axis=0, concat_axis=0, tiled=True)
        returned_flat = returned.reshape(experts * share, quarter)
        weight_of = jnp.sum(jnp.where(hit, route_weights[:, :, None], 0.0), axis=1)
        weight_hi = weight_of.astype(jnp.bfloat16)
        weight_lo = (weight_of - weight_hi.astype(jnp.float32)).astype(jnp.bfloat16)
        mixed = mixed + jnp.dot(weight_hi, returned_flat, preferred_element_type=jnp.float32)
        mixed = mixed + jnp.dot(weight_lo, returned_flat, preferred_element_type=jnp.float32)
    return mixed.astype(jnp.bfloat16)


def solution(mesh):
    in_specs = (
        P("expert", "dp"),
        P("expert", None),
        P("expert", None),
        P(),
        P("expert", "dp", None),
        P("expert", "dp", None),
        P("expert", None, "dp"),
    )
    out_specs = P("expert", "dp")
    return jax.shard_map(
        per_device, mesh=mesh, in_specs=in_specs, out_specs=out_specs, check_vma=False
    )
```

```python
import jax
import jax.numpy as jnp
from jax import lax
from jax.sharding import PartitionSpec as P

from jax.experimental import pallas as pl


def gate_up_kernel(x_ref, wg_ref, wu_ref, o_ref):
    col = pl.program_id(0)
    width = wg_ref.shape[1]
    half = width * pl.num_programs(0)
    x = x_ref[...]
    gate = jnp.dot(x, wg_ref[...], preferred_element_type=jnp.float32)
    up = jnp.dot(x, wu_ref[...], preferred_element_type=jnp.float32)
    o_ref[:, pl.ds(pl.multiple_of(col * width, width), width)] = gate.astype(o_ref.dtype)
    o_ref[:, pl.ds(pl.multiple_of(half + col * width, width), width)] = up.astype(o_ref.dtype)


def gate_up(x, wg, wu, width=256):
    rows, depth = x.shape
    hidden = wg.shape[1]
    return pl.pallas_call(
        gate_up_kernel,
        grid=(hidden // width,),
        in_specs=[
            pl.BlockSpec((rows, depth), lambda c: (0, 0)),
            pl.BlockSpec((depth, width), lambda c: (0, c)),
            pl.BlockSpec((depth, width), lambda c: (0, c)),
        ],
        out_specs=pl.BlockSpec((rows, 2 * hidden), lambda c: (0, 0)),
        out_shape=jax.ShapeDtypeStruct((rows, 2 * hidden), jnp.bfloat16),
    )(x, wg, wu)


def expert_rows(rows, w_gate, w_up, w_down, hidden):
    summed = lax.psum_scatter(
        gate_up(rows, w_gate, w_up),
        "dp",
        scatter_dimension=0,
        tiled=True,
    ).astype(jnp.float32)
    activated = (jax.nn.silu(summed[:, :hidden]) * summed[:, hidden:]).astype(jnp.bfloat16)
    results = jnp.dot(
        lax.all_gather(activated, "dp", axis=0, tiled=True),
        w_down,
        preferred_element_type=jnp.float32,
    )
    return results.astype(jnp.bfloat16)


def per_device(tokens, route_ids, route_weights, swap_flags, gate_weight, up_weight, down_weight):
    experts = lax.axis_size("expert")
    tok_rows, quarter = tokens.shape
    choices_per = route_ids.shape[1]
    hidden = gate_weight.shape[2]
    capacity = max(2, min(tok_rows, 5 * tok_rows * choices_per // (4 * experts)))
    w_gate = gate_weight[0]
    w_up = up_weight[0]
    w_down = down_weight[0]
    entries = tok_rows * choices_per
    flat_ids = route_ids.reshape(-1)
    slots = jnp.arange(experts, dtype=jnp.int32)
    onehot = flat_ids[:, None] == slots[None, :]
    entry_ids = jnp.arange(entries, dtype=jnp.int32)
    earlier = (entry_ids[:, None] > entry_ids[None, :]).astype(jnp.bfloat16)
    running = jnp.dot(earlier, onehot.astype(jnp.bfloat16), preferred_element_type=jnp.float32)
    rank_in = jnp.sum(jnp.where(onehot, running, 0.0), axis=1).astype(jnp.int32)
    flag = jnp.sum(jnp.where(onehot, swap_flags[None, :], 0), axis=1)
    home = jnp.where(flag == 1, (flat_ids + experts // 2) % experts, flat_ids)
    home = home.reshape(tok_rows, choices_per)
    rank_in = rank_in.reshape(tok_rows, choices_per)
    pieces = 2 if capacity % 2 == 0 else 1
    share = capacity // pieces
    lane = 128
    packed = (experts, share * quarter // lane, lane)
    positions = jnp.arange(experts * share, dtype=jnp.int32)
    sent = []
    hits = []
    for piece in range(pieces):
        inside = (rank_in >= piece * share) & (rank_in < (piece + 1) * share)
        slot_of = jnp.where(inside, home * share + rank_in - piece * share, -1)
        hit = slot_of[:, :, None] == positions[None, None, :]
        pick = jnp.any(hit, axis=1).astype(jnp.bfloat16)
        outgoing = lax.dot_general(
            pick, tokens, (((0,), (0,)), ((), ())), preferred_element_type=jnp.float32
        ).astype(jnp.bfloat16)
        sent.append(outgoing.reshape(packed))
        hits.append(hit)
    arrived = [
        lax.all_to_all(x, "expert", split_axis=0, concat_axis=0, tiled=True) for x in sent
    ]
    mixed = jnp.zeros((tok_rows, quarter), jnp.float32)
    for piece in range(pieces):
        served = expert_rows(
            arrived[piece].reshape(experts * share, quarter), w_gate, w_up, w_down, hidden
        ).reshape(packed)
        if piece + 1 < pieces:
            _, arrived[piece + 1] = lax.optimization_barrier((served, arrived[piece + 1]))
        returned = lax.all_to_all(served, "expert", split_axis=0, concat_axis=0, tiled=True)
        returned_flat = returned.reshape(experts * share, quarter)
        weight_of = jnp.sum(jnp.where(hits[piece], route_weights[:, :, None], 0.0), axis=1)
        weight_hi = weight_of.astype(jnp.bfloat16)
        weight_lo = (weight_of - weight_hi.astype(jnp.float32)).astype(jnp.bfloat16)
        mixed = mixed + jnp.dot(weight_hi, returned_flat, preferred_element_type=jnp.float32)
        mixed = mixed + jnp.dot(weight_lo, returned_flat, preferred_element_type=jnp.float32)
    return mixed.astype(jnp.bfloat16)


def solution(mesh):
    in_specs = (
        P("expert", "dp"),
        P("expert", None),
        P("expert", None),
        P(),
        P("expert", "dp", None),
        P("expert", "dp", None),
        P("expert", None, "dp"),
    )
    out_specs = P("expert", "dp")
    return jax.shard_map(
        per_device, mesh=mesh, in_specs=in_specs, out_specs=out_specs, check_vma=False
    )
```

```python
import jax
import jax.numpy as jnp
from jax import lax
from jax.sharding import PartitionSpec as P

from jax.experimental import pallas as pl


def gate_up_kernel(x_ref, wg_ref, wu_ref, o_ref):
    col = pl.program_id(0)
    width = wg_ref.shape[1]
    half = width * pl.num_programs(0)
    x = x_ref[...]
    gate = jnp.dot(x, wg_ref[...], preferred_element_type=jnp.float32)
    up = jnp.dot(x, wu_ref[...], preferred_element_type=jnp.float32)
    o_ref[:, pl.ds(pl.multiple_of(col * width, width), width)] = gate.astype(o_ref.dtype)
    o_ref[:, pl.ds(pl.multiple_of(half + col * width, width), width)] = up.astype(o_ref.dtype)


def gate_up(x, wg, wu, width=256):
    rows, depth = x.shape
    hidden = wg.shape[1]
    return pl.pallas_call(
        gate_up_kernel,
        grid=(hidden // width,),
        in_specs=[
            pl.BlockSpec((rows, depth), lambda c: (0, 0)),
            pl.BlockSpec((depth, width), lambda c: (0, c)),
            pl.BlockSpec((depth, width), lambda c: (0, c)),
        ],
        out_specs=pl.BlockSpec((rows, 2 * hidden), lambda c: (0, 0)),
        out_shape=jax.ShapeDtypeStruct((rows, 2 * hidden), jnp.bfloat16),
    )(x, wg, wu)


def expert_rows(rows, w_gate, w_up, w_down, hidden):
    summed = lax.psum_scatter(
        gate_up(rows, w_gate, w_up),
        "dp",
        scatter_dimension=0,
        tiled=True,
    ).astype(jnp.float32)
    activated = (jax.nn.silu(summed[:, :hidden]) * summed[:, hidden:]).astype(jnp.bfloat16)
    results = jnp.dot(
        lax.all_gather(activated, "dp", axis=0, tiled=True),
        w_down,
        preferred_element_type=jnp.float32,
    )
    return results.astype(jnp.bfloat16)


def per_device(tokens, route_ids, route_weights, swap_flags, gate_weight, up_weight, down_weight):
    experts = lax.axis_size("expert")
    tok_rows, quarter = tokens.shape
    choices_per = route_ids.shape[1]
    hidden = gate_weight.shape[2]
    capacity = max(2, min(tok_rows, 5 * tok_rows * choices_per // (4 * experts)))
    w_gate = gate_weight[0]
    w_up = up_weight[0]
    w_down = down_weight[0]
    entries = tok_rows * choices_per
    flat_ids = route_ids.reshape(-1)
    slots = jnp.arange(experts, dtype=jnp.int32)
    onehot = flat_ids[:, None] == slots[None, :]
    entry_ids = jnp.arange(entries, dtype=jnp.int32)
    earlier = (entry_ids[:, None] > entry_ids[None, :]).astype(jnp.bfloat16)
    running = jnp.dot(earlier, onehot.astype(jnp.bfloat16), preferred_element_type=jnp.float32)
    rank_in = jnp.sum(jnp.where(onehot, running, 0.0), axis=1).astype(jnp.int32)
    flag = jnp.sum(jnp.where(onehot, swap_flags[None, :], 0), axis=1)
    home = jnp.where(flag == 1, (flat_ids + experts // 2) % experts, flat_ids)
    home = home.reshape(tok_rows, choices_per)
    rank_in = rank_in.reshape(tok_rows, choices_per)
    lane = 128
    first = capacity // 16 * 16
    bounds = [(0, first), (first, capacity)] if 0 < first < capacity else [(0, capacity)]
    mixed = jnp.zeros((tok_rows, quarter), jnp.float32)
    for low, high in bounds:
        share = high - low
        if share % 16 == 0:
            layout = (experts, share, quarter)
        else:
            layout = (experts, share * quarter // lane, lane)
        positions = jnp.arange(experts * share, dtype=jnp.int32)
        inside = (rank_in >= low) & (rank_in < high)
        slot_of = jnp.where(inside, home * share + rank_in - low, -1)
        hit = slot_of[:, :, None] == positions[None, None, :]
        pick = jnp.any(hit, axis=1).astype(jnp.bfloat16)
        outgoing = lax.dot_general(
            pick, tokens, (((0,), (0,)), ((), ())), preferred_element_type=jnp.float32
        ).astype(jnp.bfloat16)
        arrived = lax.all_to_all(outgoing.reshape(layout), "expert", split_axis=0, concat_axis=0, tiled=True)
        served = expert_rows(arrived.reshape(experts * share, quarter), w_gate, w_up, w_down, hidden)
        returned = lax.all_to_all(served.reshape(layout), "expert", split_axis=0, concat_axis=0, tiled=True)
        returned_flat = returned.reshape(experts * share, quarter)
        weight_of = jnp.sum(jnp.where(hit, route_weights[:, :, None], 0.0), axis=1)
        weight_hi = weight_of.astype(jnp.bfloat16)
        weight_lo = (weight_of - weight_hi.astype(jnp.float32)).astype(jnp.bfloat16)
        mixed = mixed + jnp.dot(weight_hi, returned_flat, preferred_element_type=jnp.float32)
        mixed = mixed + jnp.dot(weight_lo, returned_flat, preferred_element_type=jnp.float32)
    return mixed.astype(jnp.bfloat16)


def solution(mesh):
    in_specs = (
        P("expert", "dp"),
        P("expert", None),
        P("expert", None),
        P(),
        P("expert", "dp", None),
        P("expert", "dp", None),
        P("expert", None, "dp"),
    )
    out_specs = P("expert", "dp")
    return jax.shard_map(
        per_device, mesh=mesh, in_specs=in_specs, out_specs=out_specs, check_vma=False
    )
```

```python
import jax
import jax.numpy as jnp
from jax import lax
from jax.sharding import PartitionSpec as P

from jax.experimental import pallas as pl


def gate_up_kernel(x_ref, wg_ref, wu_ref, o_ref):
    col = pl.program_id(0)
    width = wg_ref.shape[1]
    half = width * pl.num_programs(0)
    x = x_ref[...]
    gate = jnp.dot(x, wg_ref[...], preferred_element_type=jnp.float32)
    up = jnp.dot(x, wu_ref[...], preferred_element_type=jnp.float32)
    o_ref[:, pl.ds(pl.multiple_of(col * width, width), width)] = gate.astype(o_ref.dtype)
    o_ref[:, pl.ds(pl.multiple_of(half + col * width, width), width)] = up.astype(o_ref.dtype)


def gate_up(x, wg, wu, width=512):
    rows, depth = x.shape
    hidden = wg.shape[1]
    return pl.pallas_call(
        gate_up_kernel,
        grid=(hidden // width,),
        in_specs=[
            pl.BlockSpec((rows, depth), lambda c: (0, 0)),
            pl.BlockSpec((depth, width), lambda c: (0, c)),
            pl.BlockSpec((depth, width), lambda c: (0, c)),
        ],
        out_specs=pl.BlockSpec((rows, 2 * hidden), lambda c: (0, 0)),
        out_shape=jax.ShapeDtypeStruct((rows, 2 * hidden), jnp.bfloat16),
    )(x, wg, wu)


def expert_rows(rows, w_gate, w_up, w_down, hidden):
    summed = lax.psum_scatter(
        gate_up(rows, w_gate, w_up),
        "dp",
        scatter_dimension=0,
        tiled=True,
    ).astype(jnp.float32)
    activated = (jax.nn.silu(summed[:, :hidden]) * summed[:, hidden:]).astype(jnp.bfloat16)
    results = jnp.dot(
        lax.all_gather(activated, "dp", axis=0, tiled=True),
        w_down,
        preferred_element_type=jnp.float32,
    )
    return results.astype(jnp.bfloat16)


def per_device(tokens, route_ids, route_weights, swap_flags, gate_weight, up_weight, down_weight):
    experts = lax.axis_size("expert")
    tok_rows, quarter = tokens.shape
    choices_per = route_ids.shape[1]
    hidden = gate_weight.shape[2]
    capacity = max(2, min(tok_rows, 5 * tok_rows * choices_per // (4 * experts)))
    w_gate = gate_weight[0]
    w_up = up_weight[0]
    w_down = down_weight[0]
    entries = tok_rows * choices_per
    flat_ids = route_ids.reshape(-1)
    slots = jnp.arange(experts, dtype=jnp.int32)
    onehot = flat_ids[:, None] == slots[None, :]
    entry_ids = jnp.arange(entries, dtype=jnp.int32)
    earlier = (entry_ids[:, None] > entry_ids[None, :]).astype(jnp.bfloat16)
    running = jnp.dot(earlier, onehot.astype(jnp.bfloat16), preferred_element_type=jnp.float32)
    rank_in = jnp.sum(jnp.where(onehot, running, 0.0), axis=1).astype(jnp.int32)
    flag = jnp.sum(jnp.where(onehot, swap_flags[None, :], 0), axis=1)
    home = jnp.where(flag == 1, (flat_ids + experts // 2) % experts, flat_ids)
    home = home.reshape(tok_rows, choices_per)
    rank_in = rank_in.reshape(tok_rows, choices_per)
    pieces = 2 if capacity % 2 == 0 else 1
    share = capacity // pieces
    lane = 128
    packed = (experts, share * quarter // lane, lane)
    positions = jnp.arange(experts * share, dtype=jnp.int32)
    mixed = jnp.zeros((tok_rows, quarter), jnp.float32)
    for piece in range(pieces):
        inside = (rank_in >= piece * share) & (rank_in < (piece + 1) * share)
        slot_of = jnp.where(inside, home * share + rank_in - piece * share, -1)
        hit = slot_of[:, :, None] == positions[None, None, :]
        pick = jnp.any(hit, axis=1).astype(jnp.bfloat16)
        outgoing = lax.dot_general(
            pick, tokens, (((0,), (0,)), ((), ())), preferred_element_type=jnp.float32
        ).astype(jnp.bfloat16)
        arrived = lax.all_to_all(outgoing.reshape(packed), "expert", split_axis=0, concat_axis=0, tiled=True)
        served = expert_rows(arrived.reshape(experts * share, quarter), w_gate, w_up, w_down, hidden)
        returned = lax.all_to_all(served.reshape(packed), "expert", split_axis=0, concat_axis=0, tiled=True)
        returned_flat = returned.reshape(experts * share, quarter)
        weight_of = jnp.sum(jnp.where(hit, route_weights[:, :, None], 0.0), axis=1)
        weight_hi = weight_of.astype(jnp.bfloat16)
        weight_lo = (weight_of - weight_hi.astype(jnp.float32)).astype(jnp.bfloat16)
        mixed = mixed + jnp.dot(weight_hi, returned_flat, preferred_element_type=jnp.float32)
        mixed = mixed + jnp.dot(weight_lo, returned_flat, preferred_element_type=jnp.float32)
    return mixed.astype(jnp.bfloat16)


def solution(mesh):
    in_specs = (
        P("expert", "dp"),
        P("expert", None),
        P("expert", None),
        P(),
        P("expert", "dp", None),
        P("expert", "dp", None),
        P("expert", None, "dp"),
    )
    out_specs = P("expert", "dp")
    return jax.shard_map(
        per_device, mesh=mesh, in_specs=in_specs, out_specs=out_specs, check_vma=False
    )
```

```python
import jax
import jax.numpy as jnp
from jax import lax
from jax.sharding import PartitionSpec as P

from jax.experimental import pallas as pl


def gate_up_kernel(x_ref, wg_ref, wu_ref, o_ref):
    col = pl.program_id(0)
    width = wg_ref.shape[1]
    half = width * pl.num_programs(0)
    x = x_ref[...]
    gate = jnp.dot(x, wg_ref[...], preferred_element_type=jnp.float32)
    up = jnp.dot(x, wu_ref[...], preferred_element_type=jnp.float32)
    o_ref[:, pl.ds(pl.multiple_of(col * width, width), width)] = gate.astype(o_ref.dtype)
    o_ref[:, pl.ds(pl.multiple_of(half + col * width, width), width)] = up.astype(o_ref.dtype)


def gate_up(x, wg, wu, width=512):
    rows, depth = x.shape
    hidden = wg.shape[1]
    return pl.pallas_call(
        gate_up_kernel,
        grid=(hidden // width,),
        in_specs=[
            pl.BlockSpec((rows, depth), lambda c: (0, 0)),
            pl.BlockSpec((depth, width), lambda c: (0, c)),
            pl.BlockSpec((depth, width), lambda c: (0, c)),
        ],
        out_specs=pl.BlockSpec((rows, 2 * hidden), lambda c: (0, 0)),
        out_shape=jax.ShapeDtypeStruct((rows, 2 * hidden), jnp.bfloat16),
    )(x, wg, wu)


def expert_rows(rows, w_gate, w_up, w_down, hidden):
    summed = lax.psum_scatter(
        gate_up(rows, w_gate, w_up),
        "dp",
        scatter_dimension=0,
        tiled=True,
    ).astype(jnp.float32)
    activated = (jax.nn.silu(summed[:, :hidden]) * summed[:, hidden:]).astype(jnp.bfloat16)
    results = jnp.dot(
        lax.all_gather(activated, "dp", axis=0, tiled=True),
        w_down,
        preferred_element_type=jnp.float32,
    )
    return results.astype(jnp.bfloat16)


def per_device(tokens, route_ids, route_weights, swap_flags, gate_weight, up_weight, down_weight):
    experts = lax.axis_size("expert")
    tok_rows, quarter = tokens.shape
    choices_per = route_ids.shape[1]
    hidden = gate_weight.shape[2]
    capacity = max(2, min(tok_rows, 5 * tok_rows * choices_per // (4 * experts)))
    w_gate = gate_weight[0]
    w_up = up_weight[0]
    w_down = down_weight[0]
    entries = tok_rows * choices_per
    flat_ids = route_ids.reshape(-1)
    slots = jnp.arange(experts, dtype=jnp.int32)
    onehot = flat_ids[:, None] == slots[None, :]
    entry_ids = jnp.arange(entries, dtype=jnp.int32)
    earlier = (entry_ids[:, None] > entry_ids[None, :]).astype(jnp.bfloat16)
    running = jnp.dot(earlier, onehot.astype(jnp.bfloat16), preferred_element_type=jnp.float32)
    rank_in = jnp.sum(jnp.where(onehot, running, 0.0), axis=1).astype(jnp.int32)
    flag = jnp.sum(jnp.where(onehot, swap_flags[None, :], 0), axis=1)
    home = jnp.where(flag == 1, (flat_ids + experts // 2) % experts, flat_ids)
    home = home.reshape(tok_rows, choices_per)
    rank_in = rank_in.reshape(tok_rows, choices_per)
    lane = 128
    first = (capacity + 1) // 2 + 1 if capacity >= 4 else capacity
    bounds = [(0, first), (first, capacity)] if first < capacity else [(0, capacity)]
    mixed = jnp.zeros((tok_rows, quarter), jnp.float32)
    for low, high in bounds:
        share = high - low
        packed = (experts, share * quarter // lane, lane)
        positions = jnp.arange(experts * share, dtype=jnp.int32)
        inside = (rank_in >= low) & (rank_in < high)
        slot_of = jnp.where(inside, home * share + rank_in - low, -1)
        hit = slot_of[:, :, None] == positions[None, None, :]
        pick = jnp.any(hit, axis=1).astype(jnp.bfloat16)
        outgoing = lax.dot_general(
            pick, tokens, (((0,), (0,)), ((), ())), preferred_element_type=jnp.float32
        ).astype(jnp.bfloat16)
        arrived = lax.all_to_all(outgoing.reshape(packed), "expert", split_axis=0, concat_axis=0, tiled=True)
        served = expert_rows(arrived.reshape(experts * share, quarter), w_gate, w_up, w_down, hidden)
        returned = lax.all_to_all(served.reshape(packed), "expert", split_axis=0, concat_axis=0, tiled=True)
        returned_flat = returned.reshape(experts * share, quarter)
        weight_of = jnp.sum(jnp.where(hit, route_weights[:, :, None], 0.0), axis=1)
        weight_hi = weight_of.astype(jnp.bfloat16)
        weight_lo = (weight_of - weight_hi.astype(jnp.float32)).astype(jnp.bfloat16)
        mixed = mixed + jnp.dot(weight_hi, returned_flat, preferred_element_type=jnp.float32)
        mixed = mixed + jnp.dot(weight_lo, returned_flat, preferred_element_type=jnp.float32)
    return mixed.astype(jnp.bfloat16)


def solution(mesh):
    in_specs = (
        P("expert", "dp"),
        P("expert", None),
        P("expert", None),
        P(),
        P("expert", "dp", None),
        P("expert", "dp", None),
        P("expert", None, "dp"),
    )
    out_specs = P("expert", "dp")
    return jax.shard_map(
        per_device, mesh=mesh, in_specs=in_specs, out_specs=out_specs, check_vma=False
    )
```

```python
import jax
import jax.numpy as jnp
from jax import lax
from jax.sharding import PartitionSpec as P

from jax.experimental import pallas as pl


def gate_up_kernel(x_ref, wg_ref, wu_ref, o_ref):
    col = pl.program_id(0)
    width = wg_ref.shape[1]
    half = width * pl.num_programs(0)
    x = x_ref[...]
    gate = jnp.dot(x, wg_ref[...], preferred_element_type=jnp.float32)
    up = jnp.dot(x, wu_ref[...], preferred_element_type=jnp.float32)
    o_ref[:, pl.ds(pl.multiple_of(col * width, width), width)] = gate.astype(o_ref.dtype)
    o_ref[:, pl.ds(pl.multiple_of(half + col * width, width), width)] = up.astype(o_ref.dtype)


def gate_up(x, wg, wu, width=512):
    rows, depth = x.shape
    hidden = wg.shape[1]
    return pl.pallas_call(
        gate_up_kernel,
        grid=(hidden // width,),
        in_specs=[
            pl.BlockSpec((rows, depth), lambda c: (0, 0)),
            pl.BlockSpec((depth, width), lambda c: (0, c)),
            pl.BlockSpec((depth, width), lambda c: (0, c)),
        ],
        out_specs=pl.BlockSpec((rows, 2 * hidden), lambda c: (0, 0)),
        out_shape=jax.ShapeDtypeStruct((rows, 2 * hidden), jnp.bfloat16),
    )(x, wg, wu)


def expert_rows(rows, w_gate, w_up, w_down, hidden):
    summed = lax.psum_scatter(
        gate_up(rows, w_gate, w_up),
        "dp",
        scatter_dimension=0,
        tiled=True,
    ).astype(jnp.float32)
    activated = (jax.nn.silu(summed[:, :hidden]) * summed[:, hidden:]).astype(jnp.bfloat16)
    results = jnp.dot(
        lax.all_gather(activated, "dp", axis=0, tiled=True),
        w_down,
        preferred_element_type=jnp.float32,
    )
    return results.astype(jnp.bfloat16)


def per_device(tokens, route_ids, route_weights, swap_flags, gate_weight, up_weight, down_weight):
    experts = lax.axis_size("expert")
    tok_rows, quarter = tokens.shape
    choices_per = route_ids.shape[1]
    hidden = gate_weight.shape[2]
    capacity = max(2, min(tok_rows, 5 * tok_rows * choices_per // (4 * experts)))
    w_gate = gate_weight[0]
    w_up = up_weight[0]
    w_down = down_weight[0]
    entries = tok_rows * choices_per
    flat_ids = route_ids.reshape(-1)
    slots = jnp.arange(experts, dtype=jnp.int32)
    onehot = flat_ids[:, None] == slots[None, :]
    entry_ids = jnp.arange(entries, dtype=jnp.int32)
    earlier = (entry_ids[:, None] > entry_ids[None, :]).astype(jnp.bfloat16)
    running = jnp.dot(earlier, onehot.astype(jnp.bfloat16), preferred_element_type=jnp.float32)
    rank_in = jnp.sum(jnp.where(onehot, running, 0.0), axis=1).astype(jnp.int32)
    flag = jnp.sum(jnp.where(onehot, swap_flags[None, :], 0), axis=1)
    home = jnp.where(flag == 1, (flat_ids + experts // 2) % experts, flat_ids)
    home = home.reshape(tok_rows, choices_per)
    rank_in = rank_in.reshape(tok_rows, choices_per)
    lane = 128
    first = (capacity + 1) // 2 + 2 if capacity >= 6 else capacity
    bounds = [(0, first), (first, capacity)] if first < capacity else [(0, capacity)]
    mixed = jnp.zeros((tok_rows, quarter), jnp.float32)
    for low, high in bounds:
        share = high - low
        packed = (experts, share * quarter // lane, lane)
        positions = jnp.arange(experts * share, dtype=jnp.int32)
        inside = (rank_in >= low) & (rank_in < high)
        slot_of = jnp.where(inside, home * share + rank_in - low, -1)
        hit = slot_of[:, :, None] == positions[None, None, :]
        pick = jnp.any(hit, axis=1).astype(jnp.bfloat16)
        outgoing = lax.dot_general(
            pick, tokens, (((0,), (0,)), ((), ())), preferred_element_type=jnp.float32
        ).astype(jnp.bfloat16)
        arrived = lax.all_to_all(outgoing.reshape(packed), "expert", split_axis=0, concat_axis=0, tiled=True)
        served = expert_rows(arrived.reshape(experts * share, quarter), w_gate, w_up, w_down, hidden)
        returned = lax.all_to_all(served.reshape(packed), "expert", split_axis=0, concat_axis=0, tiled=True)
        returned_flat = returned.reshape(experts * share, quarter)
        weight_of = jnp.sum(jnp.where(hit, route_weights[:, :, None], 0.0), axis=1)
        weight_hi = weight_of.astype(jnp.bfloat16)
        weight_lo = (weight_of - weight_hi.astype(jnp.float32)).astype(jnp.bfloat16)
        mixed = mixed + jnp.dot(weight_hi, returned_flat, preferred_element_type=jnp.float32)
        mixed = mixed + jnp.dot(weight_lo, returned_flat, preferred_element_type=jnp.float32)
    return mixed.astype(jnp.bfloat16)


def solution(mesh):
    in_specs = (
        P("expert", "dp"),
        P("expert", None),
        P("expert", None),
        P(),
        P("expert", "dp", None),
        P("expert", "dp", None),
        P("expert", None, "dp"),
    )
    out_specs = P("expert", "dp")
    return jax.shard_map(
        per_device, mesh=mesh, in_specs=in_specs, out_specs=out_specs, check_vma=False
    )
```
